512 devices in a mesh: section: 4 (over x), doc: 32 (over z, core), mp: 4 (over y).
Axes of the slice: x: 4, y: 4, z: 16, core: 2. Of those that a mesh axis runs over, the one named last changes fastest.
Arguments:
- queries: bfloat16 [64, 512, 8, 4, 128], P('doc', None, 'section', 'mp'), may hold values from -420 to 420
- cotangent: bfloat16 [64, 512, 8, 4, 128], P('doc', None, 'section', 'mp'), may hold values from -180 to 180
- cache: bfloat16 [512, 128, 4, 2, 128], P('doc', 'section', 'mp'), may hold values from -7 to 7
- momentum: float32 [512, 128, 4, 2, 128], P('doc', 'section', 'mp'), may hold values from -3 to 3
- doc_lists: int32 [64, 8], P('doc'), may hold values from 0 to 511, as said below
- place: int32 [512], replicated, may hold values from 0 to 511, as said below
Outputs:
- attention: bfloat16 [64, 512, 8, 4, 128], P('doc', None, 'section', 'mp')
- new_cache: bfloat16 [512, 128, 4, 2, 128], P('doc', 'section', 'mp')
- new_momentum: float32 [512, 128, 4, 2, 128], P('doc', 'section', 'mp')
The draws below stay inside these ranges and needn't reach their ends.
Inputs may be any that keep to these rules, and one draw needn't show every extreme that they name: `doc_lists`: the 2 rows of one index of doc (an aligned block of rows) name 16 different documents in all. Counting each document's owner as place[document] // 16, those documents lie on at most 1 per owner. `place`: each row of cache holds exactly one document.
All inputs are finite; a program needn't handle non-finite values.
Results may differ from the reference program's by a relative error of at most 0.017.
Values may be sent and summed in bfloat16 or wider, within the bound.
No kernel may reach another device: no remote copies, remote signals or barrier semaphores. Data moves between devices by JAX's collectives and lax.ppermute only.
A program may use at most 64 MiB of HBM per device.

```python
import math
import jax
import jax.numpy as jnp
from jax import lax

HD = 128
GROUP = 8
KVH = 4
LEN = 128
SEQ = 512
ROWS_DEV = 2
LIST = 8
DOC_DEV = 16
ROWS = 64
DOCS = 512
N_SECTION = 4


def make_place(key):
    return jax.random.permutation(jax.random.fold_in(key, 11), DOCS).astype(jnp.int32)


def make_lists(key):
    place = make_place(key)
    inverse = jnp.argsort(place, stable=True).astype(jnp.int32)
    owners = DOCS // DOC_DEV
    readers = ROWS // ROWS_DEV
    request_total = ROWS_DEV * LIST
    owner_used = min(owners, request_total)
    shared_offset = jax.random.randint(jax.random.fold_in(key, 43), (owners,), 0, DOC_DEV, dtype=jnp.int32)

    def per_reader(reader_key, reader):
        key_a, key_b, key_c, key_d, key_e = jax.random.split(reader_key, 5)
        owner_ids = jnp.arange(owners, dtype=jnp.int32)
        random_part = jax.random.randint(key_a, (owners,), 0, 65536, dtype=jnp.int32)
        owner_lean = owner_ids * (32768 // owners)
        special = reader < 2
        target_doc = jnp.where(reader == 0, DOCS - 1, 0).astype(jnp.int32)
        target_place = place[target_doc]
        drawn_forced = owners - 1 - jax.random.randint(key_b, (), 0, max(1, owners // 4), dtype=jnp.int32)
        forced = jnp.where(special, target_place // DOC_DEV, drawn_forced).astype(jnp.int32)
        owner_score = (random_part + owner_lean) * owners + owner_ids
        owner_score = jnp.where(owner_ids == forced, 1073741824, owner_score)
        chosen = lax.top_k(owner_score, owner_used)[1].astype(jnp.int32)
        popular = jax.random.randint(key_c, (owners,), 0, 4, dtype=jnp.int32) < 3
        own_offset = jax.random.randint(key_e, (owners,), 0, DOC_DEV, dtype=jnp.int32)
        offset = jnp.where(popular, shared_offset, own_offset)
        offset = jnp.where(special & (owner_ids == forced), target_place % DOC_DEV, offset).astype(jnp.int32)
        request_ids = jnp.arange(request_total, dtype=jnp.int32)
        owner_pick = chosen[request_ids % owner_used]
        slot_index = (offset[owner_pick] + request_ids // owner_used) % DOC_DEV
        doc_ids = inverse[owner_pick * DOC_DEV + slot_index]
        shuffle = jax.random.permutation(key_d, request_total)
        return doc_ids[shuffle]
    reader_keys = jax.random.split(jax.random.fold_in(key, 41), readers)
    reader_index = jnp.arange(readers, dtype=jnp.int32)
    return jax.vmap(per_reader)(reader_keys, reader_index).reshape(ROWS, LIST).astype(jnp.int32)


def cache_values(key):
    normal_part = jnp.clip(jax.random.normal(jax.random.fold_in(key, 21), (DOCS, LEN, KVH, 2, HD), jnp.float32), -6.0, 6.0)
    return normal_part


def draw_place(key, part):
    return make_place(key)


def draw_doc_lists(key, part):
    return make_lists(key)


def draw_cache(key, part):
    return cache_values(key).astype(jnp.bfloat16)


def draw_cotangent(key, part):
    noise = jnp.clip(jax.random.normal(jax.random.fold_in(key, 51), (ROWS, SEQ, GROUP, KVH, HD), jnp.float32), -6.0, 6.0)
    values = 30.0 * noise
    return values.astype(jnp.bfloat16)


def draw_queries(key, part):
    values = jnp.clip(jax.random.normal(jax.random.fold_in(key, 31), (ROWS, SEQ, GROUP, KVH, HD), jnp.float32), -6.0, 6.0)
    return values.astype(jnp.bfloat16)


def block_scale(rng, extent, cuts, least, top_value):
    def one(position, shards_of):
        steps = jax.random.uniform(jax.random.fold_in(jax.random.fold_in(rng, 6), position), (shards_of,), jnp.float32, least / len(cuts), top_value / len(cuts))
        return jnp.repeat(jnp.exp(steps), extent[position] // shards_of).reshape((-1,) + (1,) * (len(extent) - position - 1))

    gain = one(*cuts[0])
    for cut in cuts[1:]:
        gain = gain * one(*cut)
    return gain


def gaussian(rng, shape, deviation, reach, shards=(), kind=jnp.bfloat16):
    gain = block_scale(rng, shape, shards, -0.22, 0.18) if shards else 1.0
    values = jax.random.normal(rng, shape, jnp.float32) * deviation * gain
    return jnp.minimum(jnp.maximum(values, -reach), reach).astype(kind)


def setup_inputs(seed: int = 0) -> dict:
    arg_keys = jax.random.split(jax.random.key(seed), 7)
    return {
        "queries": draw_queries(jax.random.fold_in(arg_keys[6], 71), 0),
        "cotangent": draw_cotangent(jax.random.fold_in(arg_keys[6], 71), 0),
        "cache": draw_cache(jax.random.fold_in(arg_keys[6], 71), 0),
        "momentum": gaussian(arg_keys[3], (DOCS, LEN, KVH, 2, HD), 0.5, 3.0, ((0, 32), (1, 4), (2, 4)), jnp.float32),
        "doc_lists": draw_doc_lists(jax.random.fold_in(arg_keys[6], 71), 0),
        "place": draw_place(jax.random.fold_in(arg_keys[6], 71), 0),
    }


momentum_decay = 0.9
step_rate = 0.3
clip_level = 0.5

def reference(queries, cotangent, cache, momentum, doc_lists, place):
    score_scale = 1.0 / math.sqrt(HD)
    pair_count = GROUP // N_SECTION
    positions = place[doc_lists].astype(jnp.int32)

    def row_step(grad_sum, operands):
        query_row, tangent_row, cache_rows = operands
        memory = cache[cache_rows]
        key_rows = memory[:, :, :, 0, :].reshape(LIST * LEN, KVH, HD).astype(jnp.float32)
        value_rows = memory[:, :, :, 1, :].reshape(LIST * LEN, KVH, HD).astype(jnp.float32)
        query_full = query_row.astype(jnp.float32)
        tangent_full = tangent_row.astype(jnp.float32)
        scores = jnp.einsum('sgkd,nkd->sgkn', query_full, key_rows) * score_scale
        weights = jax.nn.softmax(scores, axis=-1)
        weight_bf = lax.optimization_barrier(weights.astype(jnp.bfloat16)).astype(jnp.float32)
        attended = jnp.einsum('sgkn,nkd->sgkd', weight_bf, value_rows).astype(jnp.bfloat16)
        row_delta = lax.optimization_barrier(jnp.sum(attended.astype(jnp.float32) * tangent_full, axis=-1, keepdims=True))
        grad_weights = jnp.einsum('sgkd,nkd->sgkn', tangent_full, value_rows)
        grad_scores = (weights * (grad_weights - row_delta) * score_scale).astype(jnp.bfloat16)
        grad_scores = lax.optimization_barrier(grad_scores).astype(jnp.float32)
        block_shape = (SEQ, N_SECTION, pair_count, KVH, LIST * LEN)
        head_shape = (SEQ, N_SECTION, pair_count, KVH, HD)
        grad_keys = jnp.einsum('sbpkn,sbpkd->bnkd', grad_scores.reshape(block_shape), query_full.reshape(head_shape))
        grad_values = jnp.einsum('sbpkn,sbpkd->bnkd', weight_bf.reshape(block_shape), tangent_full.reshape(head_shape))
        blocks = jnp.stack([grad_keys, grad_values], axis=3)
        blocks = lax.optimization_barrier(blocks.astype(jnp.bfloat16)).astype(jnp.float32)
        contribution = lax.optimization_barrier(jnp.sum(blocks, axis=0)).reshape(LIST, LEN, KVH, 2, HD)
        return (grad_sum.at[cache_rows].add(contribution), attended)
    start = jnp.zeros((DOCS, LEN, KVH, 2, HD), jnp.float32)
    gradient, attention = lax.scan(row_step, start, (queries, cotangent, positions))
    norm_value = jnp.sqrt(jnp.sum(gradient * gradient))
    clip_limit = clip_level * math.sqrt(DOCS * LEN * KVH * 2 * HD)
    factor = clip_limit / jnp.maximum(norm_value, clip_limit)
    new_momentum = momentum_decay * momentum + factor * gradient
    new_cache = (cache.astype(jnp.float32) - step_rate * new_momentum).astype(jnp.bfloat16)
    return (attention, new_cache, new_momentum)
```

```python
import functools
import math

import jax
import jax.numpy as jnp
from jax import lax
from jax.experimental import pallas as pl
from jax.experimental.pallas import tpu as pltpu
from jax.sharding import PartitionSpec as P


momentum_decay = 0.9
step_rate = 0.3
clip_level = 0.5

f32 = jnp.float32
bf16 = jnp.bfloat16
NT = (((1,), (1,)), ((), ()))
NN = (((1,), (0,)), ((), ()))


def dot(a, b, dims):
    return lax.dot_general(a, b, dims, preferred_element_type=f32)


VMEM = pl.BlockSpec(memory_space=pltpu.VMEM)
SMEM = pl.BlockSpec(memory_space=pltpu.SMEM)


def pick_kernel(slot_ref, cache_ref, out_ref, split_ref):
    docs, rows, _ = cache_ref.shape
    half = rows // 2
    row = lax.broadcasted_iota(jnp.int32, (rows, rows), 0)
    col = lax.broadcasted_iota(jnp.int32, (rows, rows), 1)
    source = jnp.where(row < half, 2 * row, 2 * (row - half) + 1)
    order = jnp.where(col == source, 1.0, 0.0).astype(bf16)
    for d in range(docs):
        split_ref[d] = dot(order, cache_ref[d], NN).astype(bf16)

    def one(j, _):
        out_ref[j] = split_ref[jnp.maximum(slot_ref[j, 0, 0], 0)]
        return 0

    lax.fori_loop(0, out_ref.shape[0], one, 0)


def pick(slots, cache):
    readers = slots.shape[0]
    return pl.pallas_call(
        pick_kernel,
        out_shape=jax.ShapeDtypeStruct((readers,) + cache.shape[1:], bf16),
        in_specs=[SMEM, VMEM],
        out_specs=VMEM,
        scratch_shapes=[pltpu.VMEM(cache.shape, bf16)],
        name="pick",
    )(slots, cache)


def load_memory(table_ref, arrived_ref, key_ref, value_ref, r, list_len, part):
    for i in range(list_len):
        o = table_ref[r * list_len + i]
        key_ref[i * part : (i + 1) * part, :] = arrived_ref[o, :part, :]
        value_ref[i * part : (i + 1) * part, :] = arrived_ref[o, part:, :]


def stat_row(table_ref, requests, step, r, t, rows, tiles, sections):
    section = lax.rem(table_ref[requests] + step, sections)
    return (section * rows + r) * tiles + t


def token_refs(refs):
    q_own, t_own, prev, following, q_far, t_far = refs
    qs = (q_own.at[0], prev.at[0, 0], following.at[0, 0], q_far.at[0])
    ts = (t_own.at[0], prev.at[1, 0], following.at[1, 0], t_far.at[0])
    return qs, ts


def token_specs(width, head_size):
    one = pl.BlockSpec((1, width, head_size), lambda r, t: (r, t, 0))
    two = pl.BlockSpec((2, 1, width, head_size), lambda r, t: (0, r, t, 0))
    return one, [one, one, two, two, one, one]


def stats_kernel(list_len, part, scale2, rows, tiles, steps, table_ref, arrived_ref, *refs):
    sections = len(steps)
    q_refs, t_refs = token_refs(refs[:6])
    stats_ref, key_ref, value_ref = refs[6:]
    r, t = pl.program_id(0), pl.program_id(1)
    total = sections * rows * tiles

    @pl.when(t == 0)
    def _():
        load_memory(table_ref, arrived_ref, key_ref, value_ref, r, list_len, part)

    for step, q_ref, t_ref in zip(steps, q_refs, t_refs):
        s = dot(key_ref[...], q_ref[...], NT)
        dp = dot(value_ref[...], t_ref[...], NT)
        top = jnp.max(s, axis=0, keepdims=True)
        p = jnp.exp2((s - top) * scale2)
        index = stat_row(table_ref, rows * list_len, step, r, t, rows, tiles, sections)
        mine = (top, jnp.sum(p, axis=0, keepdims=True), jnp.sum(p * dp, axis=0, keepdims=True))
        for kind, value in enumerate(mine):
            for c in range(sections):
                stats_ref[c, pl.ds(kind * total + index, 1), :] = value


def grad_kernel(list_len, part, scale, scale2, rows, tiles, steps, table_ref, arrived_ref, stats_ref, *refs):
    sections = len(steps)
    q_refs, t_refs = token_refs(refs[:6])
    out_refs = refs[6 : 6 + sections]
    parcel_ref, key_ref, value_ref, turned_ref, total_ref, dk_ref, dv_ref = refs[6 + sections :]
    r, t = pl.program_id(0), pl.program_id(1)
    total = sections * rows * tiles

    @pl.when((r == 0) & (t == 0))
    def _():
        parcel_ref[...] = jnp.zeros_like(parcel_ref)
        tops = [stats_ref[c, :total, :] for c in range(sections)]
        top = functools.reduce(jnp.maximum, tops)
        shares = [jnp.exp2((x - top) * scale2) for x in tops]
        norm = sum(a * stats_ref[c, total : 2 * total, :] for c, a in enumerate(shares))
        dots = sum(a * stats_ref[c, 2 * total :, :] for c, a in enumerate(shares))
        inverse = 1.0 / norm
        total_ref[:total, :] = top
        total_ref[total : 2 * total, :] = inverse
        total_ref[2 * total :, :] = dots * inverse

    @pl.when(t == 0)
    def _():
        load_memory(table_ref, arrived_ref, key_ref, value_ref, r, list_len, part)
        turned_ref[...] = value_ref[...].astype(f32).T.astype(bf16)
        dk_ref[...] = jnp.zeros_like(dk_ref)
        dv_ref[...] = jnp.zeros_like(dv_ref)

    for step, q_ref, t_ref, out_ref in zip(steps, q_refs, t_refs, out_refs):
        q, tangent = q_ref[...], t_ref[...]
        index = stat_row(table_ref, rows * list_len, step, r, t, rows, tiles, sections)
        top = total_ref[pl.ds(index, 1), :]
        inverse = total_ref[pl.ds(total + index, 1), :]
        delta = total_ref[pl.ds(2 * total + index, 1), :]
        s = dot(key_ref[...], q, NT)
        w = jnp.exp2((s - top) * scale2) * inverse
        w16 = w.astype(bf16)
        out_ref[0] = dot(turned_ref[...], w16, NN).T.astype(bf16)
        dv_ref[...] += dot(w16, tangent, NN)
        dp = dot(value_ref[...], tangent, NT)
        ds = (w * (dp - delta)).astype(bf16)
        dk_ref[...] += dot(ds, q, NN)

    @pl.when(t == tiles - 1)
    def _():
        for i in range(list_len):
            o = table_ref[r * list_len + i]
            parcel_ref[o, :part, :] = (dk_ref[i * part : (i + 1) * part, :] * scale).astype(bf16)
            parcel_ref[o, part:, :] = dv_ref[i * part : (i + 1) * part, :].astype(bf16)


def row_stats(table, arrived, tensors, steps, list_len, part, width):
    rows, tokens, head_size = tensors[0].shape
    tiles, keys, sections = tokens // width, list_len * part, len(steps)
    _, token_ins = token_specs(width, head_size)
    scale2 = math.log2(math.e) / math.sqrt(head_size)
    pairs = rows * sections * tokens * keys
    return pl.pallas_call(
        functools.partial(stats_kernel, list_len, part, scale2, rows, tiles, steps),
        out_shape=jax.ShapeDtypeStruct((sections, 3 * sections * rows * tiles, width), f32),
        grid=(rows, tiles),
        in_specs=[SMEM, VMEM] + token_ins,
        out_specs=VMEM,
        scratch_shapes=[pltpu.VMEM((keys, head_size), bf16)] * 2,
        cost_estimate=pl.CostEstimate(
            flops=4 * pairs * head_size, bytes_accessed=4 * sections * tensors[0].size, transcendentals=pairs
        ),
        name="stats",
    )(table, arrived, *tensors)


def row_grads(table, arrived, stats, tensors, steps, list_len, part, width):
    rows, tokens, head_size = tensors[0].shape
    tiles, keys, sections = tokens // width, list_len * part, len(steps)
    spec, token_ins = token_specs(width, head_size)
    scale = 1.0 / math.sqrt(head_size)
    scale2 = math.log2(math.e) * scale
    pairs = rows * sections * tokens * keys
    return pl.pallas_call(
        functools.partial(grad_kernel, list_len, part, scale, scale2, rows, tiles, steps),
        out_shape=[jax.ShapeDtypeStruct(tensors[0].shape, bf16)] * sections + [jax.ShapeDtypeStruct(arrived.shape, bf16)],
        grid=(rows, tiles),
        in_specs=[SMEM, VMEM, VMEM] + token_ins,
        out_specs=[spec] * sections + [VMEM],
        scratch_shapes=[
            pltpu.VMEM((keys, head_size), bf16),
            pltpu.VMEM((keys, head_size), bf16),
            pltpu.VMEM((head_size, keys), bf16),
            pltpu.VMEM(stats.shape[1:], f32),
            pltpu.VMEM((keys, head_size), f32),
            pltpu.VMEM((keys, head_size), f32),
        ],
        cost_estimate=pl.CostEstimate(
            flops=10 * pairs * head_size, bytes_accessed=6 * sections * tensors[0].size, transcendentals=pairs
        ),
        name="grads",
    )(table, arrived, stats, *tensors)


def collect_kernel(slot_ref, returned_ref, grad_ref, square_ref):
    grad_ref[...] = jnp.zeros_like(grad_ref)

    def one(j, _):
        @pl.when(slot_ref[j, 0, 0] >= 0)
        def _():
            d = slot_ref[j, 0, 0]
            grad_ref[d] = grad_ref[d] + returned_ref[j].astype(f32)

        return 0

    lax.fori_loop(0, returned_ref.shape[0], one, 0)

    def square(d, total):
        g = grad_ref[d]
        return total + g * g

    total = lax.fori_loop(0, grad_ref.shape[0], square, jnp.zeros(grad_ref.shape[1:], f32))
    total = jnp.sum(total, axis=0, keepdims=True)
    for j in range(square_ref.shape[0]):
        square_ref[j] = total


def collect(slots, returned, docs):
    return pl.pallas_call(
        collect_kernel,
        out_shape=(
            jax.ShapeDtypeStruct((docs,) + returned.shape[1:], f32),
            jax.ShapeDtypeStruct((returned.shape[0], 1, returned.shape[2]), f32),
        ),
        in_specs=[SMEM, VMEM],
        out_specs=(VMEM, VMEM),
        name="collect",
    )(slots, returned)


def fold_kernel(square_ref, out_ref):
    total = functools.reduce(jnp.add, [square_ref[j] for j in range(square_ref.shape[0])])
    for j in range(out_ref.shape[0]):
        out_ref[j] = total


def fold(square, count):
    return pl.pallas_call(
        fold_kernel,
        out_shape=jax.ShapeDtypeStruct((count,) + square.shape[1:], f32),
        in_specs=[VMEM],
        out_specs=VMEM,
        name="fold",
    )(square)


def update_kernel(clip_limit, square_ref, grad_ref, cache_ref, momentum_ref, new_cache_ref, new_momentum_ref):
    total = functools.reduce(jnp.add, [square_ref[j] for j in range(square_ref.shape[0])])
    norm = jnp.sqrt(jnp.sum(total, axis=1, keepdims=True))
    factor = clip_limit / jnp.maximum(norm, clip_limit)
    docs, rows, _ = grad_ref.shape
    half = rows // 2

    def one(d, _):
        for kind in range(2):
            at = (d, pl.ds(kind, half, stride=2), slice(None))
            new_momentum_ref[at] = momentum_decay * momentum_ref[at] + factor * grad_ref[d, kind * half : (kind + 1) * half, :]
        new_cache_ref[d] = (cache_ref[d].astype(f32) - step_rate * new_momentum_ref[d]).astype(bf16)
        return 0

    lax.fori_loop(0, docs, one, 0)


def update(clip_limit, square, grad, cache, momentum):
    return pl.pallas_call(
        functools.partial(update_kernel, clip_limit),
        out_shape=(jax.ShapeDtypeStruct(cache.shape, bf16), jax.ShapeDtypeStruct(momentum.shape, f32)),
        in_specs=[VMEM] * 4,
        out_specs=(VMEM, VMEM),
        name="update",
    )(square, grad, cache, momentum)


def swap(x, axes):
    return lax.all_to_all(x, axes, split_axis=0, concat_axis=0, tiled=True)


def pass_on(x, ring):
    return lax.ppermute(x, "section", ring)


def body(queries, cotangent, cache, momentum, doc_lists, place):
    rows_dev, seq_len, head_count, kv_count, head_size = queries.shape
    doc_dev, len_part = cache.shape[:2]
    doc_total = place.shape[0]
    owners = doc_total // doc_dev
    list_len = doc_lists.shape[1]
    requests = rows_dev * list_len
    sections = lax.axis_size("section")
    tokens = seq_len * head_count

    q_own = queries.reshape(rows_dev, tokens, head_size)
    t_own = cotangent.reshape(rows_dev, tokens, head_size)
    up = [(i, (i + 1) % sections) for i in range(sections)]
    down = [(i, (i - 1) % sections) for i in range(sections)]
    across = [(i, (i + 2) % sections) for i in range(sections)]
    both = jnp.stack([q_own, t_own])
    prev, following = pass_on(both, up), pass_on(both, down)
    q_far, t_far = pass_on(prev[0], up), pass_on(following[1], down)
    tensors = (q_own, t_own, prev, following, q_far, t_far)
    steps = (0, 3, 1, 2)

    lists = doc_lists.reshape(requests)
    named = lists[:, None] == jnp.arange(doc_total, dtype=jnp.int32)[None, :]
    positions = jnp.sum(jnp.where(named, place[None, :], 0), axis=1)
    holder = positions // doc_dev
    wanted = jnp.sum(
        jnp.where(holder[None, :] == jnp.arange(owners, dtype=jnp.int32)[:, None], positions[None, :] % doc_dev + 1, 0),
        axis=1,
    ) - 1
    slots = swap(wanted.reshape(owners, 1, 1), "doc")

    stored = cache.reshape(doc_dev, len_part * 2, head_size)
    outgoing = pick(slots, stored)
    arrived = swap(outgoing, "doc")

    width = 512
    table = jnp.concatenate([holder, lax.axis_index("section").reshape(1).astype(jnp.int32)])
    stats = swap(row_stats(table, arrived, tensors, steps, list_len, len_part, width), "section")
    own, to_prev, to_next, to_far, parcel = row_grads(table, arrived, stats, tensors, steps, list_len, len_part, width)
    shares = (own, pass_on(to_prev, down), pass_on(to_next, up), pass_on(to_far, across))
    attention = sum(x.astype(f32) for x in shares).astype(bf16).reshape(queries.shape)

    returned = swap(parcel, "doc")
    gradient, square = collect(slots, returned, doc_dev)
    planes = sections * lax.axis_size("mp")
    square = fold(swap(square, "doc"), planes)
    square = swap(square, ("section", "mp"))
    entry_count = doc_total * len_part * planes * kv_count * 2 * head_size
    clip_limit = clip_level * math.sqrt(entry_count)
    new_cache, new_momentum = update(
        clip_limit, square, gradient, stored, momentum.reshape(doc_dev, len_part * 2, head_size)
    )
    return (attention, new_cache.reshape(cache.shape), new_momentum.reshape(momentum.shape))


def solution(mesh):
    in_specs = (
        P("doc", None, "section", "mp", None),
        P("doc", None, "section", "mp", None),
        P("doc", "section", "mp", None, None),
        P("doc", "section", "mp", None, None),
        P("doc", None),
        P(),
    )
    out_specs = (
        P("doc", None, "section", "mp", None),
        P("doc", "section", "mp", None, None),
        P("doc", "section", "mp", None, None),
    )

    return jax.shard_map(body, mesh=mesh, in_specs=in_specs, out_specs=out_specs, check_vma=False)
```

```python
import functools
import math

import jax
import jax.numpy as jnp
from jax import lax
from jax.experimental import pallas as pl
from jax.experimental.pallas import tpu as pltpu
from jax.sharding import PartitionSpec as P


momentum_decay = 0.9
step_rate = 0.3
clip_level = 0.5

f32 = jnp.float32
bf16 = jnp.bfloat16
NT = (((1,), (1,)), ((), ()))
NN = (((1,), (0,)), ((), ()))


def dot(a, b, dims):
    return lax.dot_general(a, b, dims, preferred_element_type=f32)


VMEM = pl.BlockSpec(memory_space=pltpu.VMEM)
SMEM = pl.BlockSpec(memory_space=pltpu.SMEM)


def small(mib):
    return pltpu.CompilerParams(vmem_limit_bytes=mib << 20)


def ask_kernel(doc_dev, list_ref, place_ref, wanted_ref, table_ref):
    for o in range(wanted_ref.shape[0]):
        wanted_ref[o, 0, 0] = -1
    rows, list_len = list_ref.shape
    for i in range(rows * list_len):
        position = place_ref[list_ref[i // list_len, i % list_len]]
        holder = lax.div(position, doc_dev)
        table_ref[i] = holder
        wanted_ref[holder, 0, 0] = lax.rem(position, doc_dev)
    table_ref[rows * list_len] = lax.axis_index("section").astype(jnp.int32)


def ask(doc_lists, place, owners, doc_dev):
    return pl.pallas_call(
        functools.partial(ask_kernel, doc_dev),
        out_shape=(
            jax.ShapeDtypeStruct((owners, 1, 1), jnp.int32),
            jax.ShapeDtypeStruct((doc_lists.size + 1,), jnp.int32),
        ),
        in_specs=[SMEM, SMEM],
        out_specs=(SMEM, SMEM),
        name="ask",
    )(doc_lists, place)


def split_kernel(cache_ref, split_ref):
    docs, rows, _ = cache_ref.shape
    half = rows // 2
    row = lax.broadcasted_iota(jnp.int32, (rows, rows), 0)
    col = lax.broadcasted_iota(jnp.int32, (rows, rows), 1)
    source = jnp.where(row < half, 2 * row, 2 * (row - half) + 1)
    order = jnp.where(col == source, 1.0, 0.0).astype(bf16)
    for d in range(docs):
        split_ref[d] = dot(order, cache_ref[d], NN).astype(bf16)


def split(cache):
    return pl.pallas_call(
        split_kernel,
        out_shape=jax.ShapeDtypeStruct(cache.shape, bf16),
        in_specs=[VMEM],
        out_specs=VMEM,
        compiler_params=small(4),
        name="split",
    )(cache)


def pick_kernel(slot_ref, split_ref, out_ref):
    for j in range(out_ref.shape[0]):
        out_ref[j] = split_ref[jnp.maximum(slot_ref[j, 0, 0], 0)]


def pick(slots, blocks):
    return pl.pallas_call(
        pick_kernel,
        out_shape=jax.ShapeDtypeStruct((slots.shape[0],) + blocks.shape[1:], bf16),
        in_specs=[SMEM, VMEM],
        out_specs=VMEM,
        compiler_params=small(4),
        name="pick",
    )(slots, blocks)


def load_memory(table_ref, arrived_ref, key_ref, value_ref, r, list_len, part):
    for i in range(list_len):
        o = table_ref[r * list_len + i]
        key_ref[i * part : (i + 1) * part, :] = arrived_ref[o, :part, :]
        value_ref[i * part : (i + 1) * part, :] = arrived_ref[o, part:, :]


def stat_row(table_ref, requests, step, r, t, rows, tiles, sections):
    section = lax.rem(table_ref[requests] + step, sections)
    return (section * rows + r) * tiles + t


def stats_kernel(list_len, part, scale2, rows, tiles, steps, table_ref, arrived_ref, *refs):
    sections = len(steps)
    q_refs, t_refs = refs[:sections], refs[sections : 2 * sections]
    stats_ref, key_ref, value_ref = refs[2 * sections :]
    r, t = pl.program_id(0), pl.program_id(1)
    total = sections * rows * tiles

    @pl.when(t == 0)
    def _():
        load_memory(table_ref, arrived_ref, key_ref, value_ref, r, list_len, part)

    for step, q_ref, t_ref in zip(steps, q_refs, t_refs):
        s = dot(key_ref[...], q_ref[0], NT)
        dp = dot(value_ref[...], t_ref[0], NT)
        raw = jnp.max(s, axis=0, keepdims=True)
        p = jnp.exp2((s - raw) * scale2)
        top = raw * scale2
        index = stat_row(table_ref, rows * list_len, step, r, t, rows, tiles, sections)
        mine = (top, jnp.sum(p, axis=0, keepdims=True), jnp.sum(p * dp, axis=0, keepdims=True))
        for kind, value in enumerate(mine):
            for c in range(sections):
                stats_ref[c, pl.ds(kind * total + index, 1), :] = value


def grad_kernel(list_len, part, scale, scale2, rows, tiles, steps, table_ref, arrived_ref, stats_ref, *refs):
    sections = len(steps)
    q_refs, t_refs = refs[:sections], refs[sections : 2 * sections]
    parcel_ref, total_ref, key_ref, value_ref, dk_ref, dv_ref = refs[2 * sections :]
    r, t = pl.program_id(0), pl.program_id(1)
    total = sections * rows * tiles

    @pl.when((r == 0) & (t == 0))
    def _():
        parcel_ref[...] = jnp.zeros_like(parcel_ref)
        tops = [stats_ref[c, :total, :] for c in range(sections)]
        top = functools.reduce(jnp.maximum, tops)
        shares = [jnp.exp2(x - top) for x in tops]
        norm = sum(a * stats_ref[c, total : 2 * total, :] for c, a in enumerate(shares))
        dots = sum(a * stats_ref[c, 2 * total :, :] for c, a in enumerate(shares))
        total_ref[:total, :] = top + jnp.log2(norm)
        total_ref[total:, :] = dots / norm

    @pl.when(t == 0)
    def _():
        load_memory(table_ref, arrived_ref, key_ref, value_ref, r, list_len, part)
        dk_ref[...] = jnp.zeros_like(dk_ref)
        dv_ref[...] = jnp.zeros_like(dv_ref)

    for step, q_ref, t_ref in zip(steps, q_refs, t_refs):
        q, tangent = q_ref[0], t_ref[0]
        index = stat_row(table_ref, rows * list_len, step, r, t, rows, tiles, sections)
        shift = total_ref[pl.ds(index, 1), :]
        delta = total_ref[pl.ds(total + index, 1), :]
        s = dot(key_ref[...], q, NT)
        dp = dot(value_ref[...], tangent, NT)
        w = jnp.exp2(s * scale2 - shift)
        w16 = w.astype(bf16)
        ds = (w * (dp - delta)).astype(bf16)
        dv_ref[...] += dot(w16, tangent, NN)
        dk_ref[...] += dot(ds, q, NN)

    @pl.when(t == tiles - 1)
    def _():
        for i in range(list_len):
            o = table_ref[r * list_len + i]
            parcel_ref[o, :part, :] = (dk_ref[i * part : (i + 1) * part, :] * scale).astype(bf16)
            parcel_ref[o, part:, :] = dv_ref[i * part : (i + 1) * part, :].astype(bf16)


def attend_kernel(list_len, part, scale2, rows, tiles, steps, table_ref, arrived_ref, total_ref, *refs):
    sections = len(steps)
    q_refs, out_refs = refs[:sections], refs[sections : 2 * sections]
    key_ref, value_ref, turned_ref = refs[2 * sections :]
    r, t = pl.program_id(0), pl.program_id(1)

    @pl.when(t == 0)
    def _():
        load_memory(table_ref, arrived_ref, key_ref, value_ref, r, list_len, part)
        turned_ref[...] = value_ref[...].astype(f32).T.astype(bf16)

    for step, q_ref, out_ref in zip(steps, q_refs, out_refs):
        index = stat_row(table_ref, rows * list_len, step, r, t, rows, tiles, sections)
        s = dot(key_ref[...], q_ref[0], NT)
        w16 = jnp.exp2(s * scale2 - total_ref[pl.ds(index, 1), :]).astype(bf16)
        out_ref[0] = dot(turned_ref[...], w16, NN).T.astype(bf16)


def plan(qs, list_len, part, width):
    rows, tokens, head_size = qs[0].shape
    scale = 1.0 / math.sqrt(head_size)
    spec = pl.BlockSpec((1, width, head_size), lambda r, t: (r, t, 0))
    pairs = rows * len(qs) * tokens * list_len * part
    return rows, tokens // width, head_size, list_len * part, scale, math.log2(math.e) * scale, spec, pairs


def cost(pairs, head_size, dots, tensors):
    return pl.CostEstimate(
        flops=2 * dots * pairs * head_size, bytes_accessed=2 * sum(x.size for x in tensors), transcendentals=pairs
    )


def row_stats(table, arrived, qs, ts, steps, list_len, part, width):
    rows, tiles, head_size, keys, _, scale2, spec, pairs = plan(qs, list_len, part, width)
    sections = len(steps)
    return pl.pallas_call(
        functools.partial(stats_kernel, list_len, part, scale2, rows, tiles, steps),
        out_shape=jax.ShapeDtypeStruct((sections, 3 * sections * rows * tiles, width), f32),
        grid=(rows, tiles),
        in_specs=[SMEM, VMEM] + [spec] * (2 * sections),
        out_specs=VMEM,
        scratch_shapes=[pltpu.VMEM((keys, head_size), bf16)] * 2,
        cost_estimate=cost(pairs, head_size, 2, qs + ts),
        name="stats",
    )(table, arrived, *qs, *ts)


def row_grads(table, arrived, stats, qs, ts, steps, list_len, part, width):
    rows, tiles, head_size, keys, scale, scale2, spec, pairs = plan(qs, list_len, part, width)
    sections = len(steps)
    return pl.pallas_call(
        functools.partial(grad_kernel, list_len, part, scale, scale2, rows, tiles, steps),
        out_shape=(
            jax.ShapeDtypeStruct(arrived.shape, bf16),
            jax.ShapeDtypeStruct((2 * sections * rows * tiles, width), f32),
        ),
        grid=(rows, tiles),
        in_specs=[SMEM, VMEM, VMEM] + [spec] * (2 * sections),
        out_specs=(VMEM, VMEM),
        scratch_shapes=[pltpu.VMEM((keys, head_size), bf16)] * 2 + [pltpu.VMEM((keys, head_size), f32)] * 2,
        cost_estimate=cost(pairs, head_size, 4, qs + ts),
        name="grads",
    )(table, arrived, stats, *qs, *ts)


def row_attend(table, arrived, totals, qs, steps, list_len, part, width):
    rows, tiles, head_size, keys, _, scale2, spec, pairs = plan(qs, list_len, part, width)
    sections = len(steps)
    return pl.pallas_call(
        functools.partial(attend_kernel, list_len, part, scale2, rows, tiles, steps),
        out_shape=[jax.ShapeDtypeStruct(qs[0].shape, bf16)] * sections,
        grid=(rows, tiles),
        in_specs=[SMEM, VMEM, VMEM] + [spec] * sections,
        out_specs=[spec] * sections,
        scratch_shapes=[pltpu.VMEM((keys, head_size), bf16)] * 2 + [pltpu.VMEM((head_size, keys), bf16)],
        cost_estimate=cost(pairs, head_size, 2, qs + qs),
        name="attend",
    )(table, arrived, totals, *qs)


def collect_kernel(slot_ref, returned_ref, grad_ref, square_ref):
    step = pl.program_id(0)
    group = returned_ref.shape[0]

    @pl.when(step == 0)
    def _():
        grad_ref[...] = jnp.zeros_like(grad_ref)

    for j in range(group):
        d = slot_ref[step * group + j, 0, 0]

        @pl.when(d >= 0)
        def _():
            grad_ref[d] = grad_ref[d] + returned_ref[j].astype(f32)

    @pl.when(step == pl.num_programs(0) - 1)
    def _():
        total = functools.reduce(jnp.add, [grad_ref[d] * grad_ref[d] for d in range(grad_ref.shape[0])])
        total = jnp.sum(total, axis=0, keepdims=True)
        for j in range(square_ref.shape[0]):
            square_ref[j] = total


def collect(slots, returned, docs):
    readers, rows, lanes = returned.shape
    group = max(1, readers // 4)
    return pl.pallas_call(
        collect_kernel,
        out_shape=(
            jax.ShapeDtypeStruct((docs, rows, lanes), f32),
            jax.ShapeDtypeStruct((readers, 1, lanes), f32),
        ),
        grid=(readers // group,),
        in_specs=[SMEM, pl.BlockSpec((group, rows, lanes), lambda i: (i, 0, 0))],
        out_specs=(VMEM, VMEM),
        compiler_params=small(8),
        name="collect",
    )(slots, returned)


def fold_kernel(square_ref, out_ref):
    total = functools.reduce(jnp.add, [square_ref[j] for j in range(square_ref.shape[0])])
    for j in range(out_ref.shape[0]):
        out_ref[j] = total


def fold(square, count):
    return pl.pallas_call(
        fold_kernel,
        out_shape=jax.ShapeDtypeStruct((count,) + square.shape[1:], f32),
        in_specs=[VMEM],
        out_specs=VMEM,
        compiler_params=small(2),
        name="fold",
    )(square)


def update_kernel(clip_limit, square_ref, grad_ref, cache_ref, momentum_ref, new_cache_ref, new_momentum_ref):
    total = functools.reduce(jnp.add, [square_ref[j] for j in range(square_ref.shape[0])])
    norm = jnp.sqrt(jnp.sum(total, axis=1, keepdims=True))
    factor = clip_limit / jnp.maximum(norm, clip_limit)
    docs, rows, _ = grad_ref.shape
    half = rows // 2

    def one(d, _):
        for kind in range(2):
            at = (d, pl.ds(kind, half, stride=2), slice(None))
            new_momentum_ref[at] = momentum_decay * momentum_ref[at] + factor * grad_ref[d, kind * half : (kind + 1) * half, :]
        new_cache_ref[d] = (cache_ref[d].astype(f32) - step_rate * new_momentum_ref[d]).astype(bf16)
        return 0

    lax.fori_loop(0, docs, one, 0)


def update(clip_limit, square, grad, cache, momentum):
    return pl.pallas_call(
        functools.partial(update_kernel, clip_limit),
        out_shape=(jax.ShapeDtypeStruct(cache.shape, bf16), jax.ShapeDtypeStruct(momentum.shape, f32)),
        in_specs=[VMEM] * 4,
        out_specs=(VMEM, VMEM),
        compiler_params=small(8),
        name="update",
    )(square, grad, cache, momentum)


def swap(x, axes):
    return lax.all_to_all(x, axes, split_axis=0, concat_axis=0, tiled=True)


def pass_on(x, ring):
    return lax.ppermute(x, "section", ring)


def body(queries, cotangent, cache, momentum, doc_lists, place):
    rows_dev, seq_len, head_count, kv_count, head_size = queries.shape
    doc_dev, len_part = cache.shape[:2]
    doc_total = place.shape[0]
    owners = doc_total // doc_dev
    list_len = doc_lists.shape[1]
    sections = lax.axis_size("section")
    tokens = seq_len * head_count

    q_own = queries.reshape(rows_dev, tokens, head_size)
    t_own = cotangent.reshape(rows_dev, tokens, head_size)
    up = [(i, (i + 1) % sections) for i in range(sections)]
    down = [(i, (i - 1) % sections) for i in range(sections)]
    across = [(i, (i + 2) % sections) for i in range(sections)]
    q_prev, t_next = pass_on(q_own, up), pass_on(t_own, down)
    q_next, t_prev = pass_on(q_own, down), pass_on(t_own, up)
    q_far, t_far = pass_on(q_prev, up), pass_on(t_next, down)
    qs, ts = (q_own, q_prev, q_next, q_far), (t_own, t_prev, t_next, t_far)
    steps = (0, 3, 1, 2)

    wanted, table = ask(doc_lists, place, owners, doc_dev)
    slots = swap(wanted, "doc")
    stored = cache.reshape(doc_dev, len_part * 2, head_size)
    outgoing = pick(slots, split(stored))
    arrived = swap(outgoing, "doc")

    width = 512
    stats = swap(row_stats(table, arrived, qs, ts, steps, list_len, len_part, width), "section")
    parcel, totals = row_grads(table, arrived, stats, qs, ts, steps, list_len, len_part, width)
    own, to_prev, to_next, to_far = row_attend(table, arrived, totals, qs, steps, list_len, len_part, width)
    shares = (own, pass_on(to_prev, down), pass_on(to_next, up), pass_on(to_far, across))
    attention = sum(x.astype(f32) for x in shares).astype(bf16).reshape(queries.shape)

    returned = swap(parcel, "doc")
    gradient, square = collect(slots, returned, doc_dev)
    planes = sections * lax.axis_size("mp")
    square = fold(swap(square, "doc"), planes)
    square = swap(square, ("section", "mp"))
    entry_count = doc_total * len_part * planes * kv_count * 2 * head_size
    clip_limit = clip_level * math.sqrt(entry_count)
    new_cache, new_momentum = update(
        clip_limit, square, gradient, stored, momentum.reshape(doc_dev, len_part * 2, head_size)
    )
    return (attention, new_cache.reshape(cache.shape), new_momentum.reshape(momentum.shape))


def solution(mesh):
    in_specs = (
        P("doc", None, "section", "mp", None),
        P("doc", None, "section", "mp", None),
        P("doc", "section", "mp", None, None),
        P("doc", "section", "mp", None, None),
        P("doc", None),
        P(),
    )
    out_specs = (
        P("doc", None, "section", "mp", None),
        P("doc", "section", "mp", None, None),
        P("doc", "section", "mp", None, None),
    )

    return jax.shard_map(body, mesh=mesh, in_specs=in_specs, out_specs=out_specs, check_vma=False)
```

```python
import functools
import math

import jax
import jax.numpy as jnp
from jax import lax
from jax.experimental import pallas as pl
from jax.experimental.pallas import tpu as pltpu
from jax.sharding import PartitionSpec as P


momentum_decay = 0.9
step_rate = 0.3
clip_level = 0.5

f32 = jnp.float32
bf16 = jnp.bfloat16
NT = (((1,), (1,)), ((), ()))
NN = (((1,), (0,)), ((), ()))


def dot(a, b, dims):
    return lax.dot_general(a, b, dims, preferred_element_type=f32)


VMEM = pl.BlockSpec(memory_space=pltpu.VMEM)
SMEM = pl.BlockSpec(memory_space=pltpu.SMEM)


def small(mib):
    return pltpu.CompilerParams(vmem_limit_bytes=mib << 20)


def ask_kernel(doc_dev, list_ref, place_ref, wanted_ref, table_ref):
    for o in range(wanted_ref.shape[0]):
        wanted_ref[o, 0, 0] = -1
    rows, list_len = list_ref.shape
    for i in range(rows * list_len):
        position = place_ref[list_ref[i // list_len, i % list_len]]
        holder = lax.div(position, doc_dev)
        table_ref[i] = holder
        wanted_ref[holder, 0, 0] = lax.rem(position, doc_dev)
    table_ref[rows * list_len] = lax.axis_index("section").astype(jnp.int32)


def ask(doc_lists, place, owners, doc_dev):
    return pl.pallas_call(
        functools.partial(ask_kernel, doc_dev),
        out_shape=(
            jax.ShapeDtypeStruct((owners, 1, 1), jnp.int32),
            jax.ShapeDtypeStruct((doc_lists.size + 1,), jnp.int32),
        ),
        in_specs=[SMEM, SMEM],
        out_specs=(SMEM, SMEM),
        name="ask",
    )(doc_lists, place)


def split_kernel(cache_ref, split_ref):
    docs, rows, _ = cache_ref.shape
    half = rows // 2
    row = lax.broadcasted_iota(jnp.int32, (rows, rows), 0)
    col = lax.broadcasted_iota(jnp.int32, (rows, rows), 1)
    source = jnp.where(row < half, 2 * row, 2 * (row - half) + 1)
    order = jnp.where(col == source, 1.0, 0.0).astype(bf16)
    for d in range(docs):
        split_ref[d] = dot(order, cache_ref[d], NN).astype(bf16)


def split(cache):
    return pl.pallas_call(
        split_kernel,
        out_shape=jax.ShapeDtypeStruct(cache.shape, bf16),
        in_specs=[VMEM],
        out_specs=VMEM,
        compiler_params=small(4),
        name="split",
    )(cache)


def pick_kernel(slot_ref, split_ref, out_ref):
    for j in range(out_ref.shape[0]):
        out_ref[j] = split_ref[jnp.maximum(slot_ref[j, 0, 0], 0)]


def pick(slots, blocks):
    return pl.pallas_call(
        pick_kernel,
        out_shape=jax.ShapeDtypeStruct((slots.shape[0],) + blocks.shape[1:], bf16),
        in_specs=[SMEM, VMEM],
        out_specs=VMEM,
        compiler_params=small(4),
        name="pick",
    )(slots, blocks)


def load_memory(table_ref, arrived_ref, key_ref, value_ref, r, list_len, part):
    for i in range(list_len):
        o = table_ref[r * list_len + i]
        key_ref[i * part : (i + 1) * part, :] = arrived_ref[o, :part, :]
        value_ref[i * part : (i + 1) * part, :] = arrived_ref[o, part:, :]


def stat_row(table_ref, requests, step, r, t, rows, tiles, sections):
    section = lax.rem(table_ref[requests] + step, sections)
    return (section * rows + r) * tiles + t


def tile_stats(all_ref, table_ref, key_ref, value_ref, q, t, scale2, step, r, n, rows, tiles, sections, requests):
    total = sections * rows * tiles
    s = dot(key_ref[...], q, NT)
    dp = dot(value_ref[...], t, NT)
    raw = jnp.max(s, axis=0, keepdims=True)
    p = jnp.exp2((s - raw) * scale2)
    index = stat_row(table_ref, requests, step, r, n, rows, tiles, sections)
    all_ref[pl.ds(index, 1), :] = raw * scale2
    all_ref[pl.ds(total + index, 1), :] = jnp.sum(p, axis=0, keepdims=True)
    all_ref[pl.ds(2 * total + index, 1), :] = jnp.sum(p * dp, axis=0, keepdims=True)


def stats_kernel(list_len, part, scale2, rows, width, sections, steps, table_ref, arrived_ref, *refs):
    count = len(steps)
    q_refs, t_refs = refs[:count], refs[count : 2 * count]
    all_ref, key_ref, value_ref = refs[2 * count :]
    r = pl.program_id(0)
    tiles = q_refs[0].shape[1] // width
    load_memory(table_ref, arrived_ref, key_ref, value_ref, r, list_len, part)
    for step, q_ref, t_ref in zip(steps, q_refs, t_refs):
        for n in range(tiles):
            at = slice(n * width, (n + 1) * width)
            tile_stats(
                all_ref, table_ref, key_ref, value_ref, q_ref[0, at, :], t_ref[0, at, :],
                scale2, step, r, n, rows, tiles, sections, rows * list_len,
            )


def far_kernel(
    list_len, part, scale2, width, sections, step, table_ref, arrived_ref, near_ref, q_hbm, t_hbm,
    stats_ref, all_ref, key_ref, value_ref, q_ref, t_ref, sem,
):
    rows = q_hbm.shape[0]
    tiles = q_hbm.shape[1] // width
    copies = [
        [
            pltpu.make_async_copy(x.at[r], y.at[r], sem.at[r, n])
            for n, (x, y) in enumerate(((q_hbm, q_ref), (t_hbm, t_ref)))
        ]
        for r in range(rows)
    ]
    for pair in copies:
        for copy in pair:
            copy.start()
    all_ref[...] = near_ref[...]
    for r in range(rows):
        load_memory(table_ref, arrived_ref, key_ref.at[r], value_ref.at[r], r, list_len, part)
    for r in range(rows):
        for copy in copies[r]:
            copy.wait()
        for n in range(tiles):
            at = slice(n * width, (n + 1) * width)
            tile_stats(
                all_ref, table_ref, key_ref.at[r], value_ref.at[r], q_ref[r, at, :], t_ref[r, at, :],
                scale2, step, r, n, rows, tiles, sections, rows * list_len,
            )
    for c in range(sections):
        stats_ref[c] = all_ref[...]


def grad_kernel(list_len, part, scale, scale2, rows, tiles, steps, table_ref, arrived_ref, stats_ref, *refs):
    sections = len(steps)
    q_refs, t_refs = refs[:sections], refs[sections : 2 * sections]
    parcel_ref, total_ref, key_ref, value_ref, dk_ref, dv_ref = refs[2 * sections :]
    r, t = pl.program_id(0), pl.program_id(1)
    total = sections * rows * tiles

    @pl.when((r == 0) & (t == 0))
    def _():
        parcel_ref[...] = jnp.zeros_like(parcel_ref)
        tops = [stats_ref[c, :total, :] for c in range(sections)]
        top = functools.reduce(jnp.maximum, tops)
        shares = [jnp.exp2(x - top) for x in tops]
        norm = sum(a * stats_ref[c, total : 2 * total, :] for c, a in enumerate(shares))
        dots = sum(a * stats_ref[c, 2 * total :, :] for c, a in enumerate(shares))
        total_ref[:total, :] = top + jnp.log2(norm)
        total_ref[total:, :] = dots / norm

    @pl.when(t == 0)
    def _():
        load_memory(table_ref, arrived_ref, key_ref, value_ref, r, list_len, part)
        dk_ref[...] = jnp.zeros_like(dk_ref)
        dv_ref[...] = jnp.zeros_like(dv_ref)

    for step, q_ref, t_ref in zip(steps, q_refs, t_refs):
        q, tangent = q_ref[0], t_ref[0]
        index = stat_row(table_ref, rows * list_len, step, r, t, rows, tiles, sections)
        shift = total_ref[pl.ds(index, 1), :]
        delta = total_ref[pl.ds(total + index, 1), :]
        s = dot(key_ref[...], q, NT)
        dp = dot(value_ref[...], tangent, NT)
        w = jnp.exp2(s * scale2 - shift)
        w16 = w.astype(bf16)
        ds = (w * (dp - delta)).astype(bf16)
        dv_ref[...] += dot(w16, tangent, NN)
        dk_ref[...] += dot(ds, q, NN)

    @pl.when(t == tiles - 1)
    def _():
        for i in range(list_len):
            o = table_ref[r * list_len + i]
            parcel_ref[o, :part, :] = (dk_ref[i * part : (i + 1) * part, :] * scale).astype(bf16)
            parcel_ref[o, part:, :] = dv_ref[i * part : (i + 1) * part, :].astype(bf16)


def attend_kernel(list_len, part, scale2, rows, tiles, steps, table_ref, arrived_ref, total_ref, *refs):
    sections = len(steps)
    q_refs, out_refs = refs[:sections], refs[sections : 2 * sections]
    key_ref, value_ref, turned_ref = refs[2 * sections :]
    r, t = pl.program_id(0), pl.program_id(1)

    @pl.when(t == 0)
    def _():
        load_memory(table_ref, arrived_ref, key_ref, value_ref, r, list_len, part)
        turned_ref[...] = value_ref[...].astype(f32).T.astype(bf16)

    for step, q_ref, out_ref in zip(steps, q_refs, out_refs):
        index = stat_row(table_ref, rows * list_len, step, r, t, rows, tiles, sections)
        s = dot(key_ref[...], q_ref[0], NT)
        w16 = jnp.exp2(s * scale2 - total_ref[pl.ds(index, 1), :]).astype(bf16)
        out_ref[0] = dot(turned_ref[...], w16, NN).T.astype(bf16)


def plan(qs, list_len, part, width):
    rows, tokens, head_size = qs[0].shape
    scale = 1.0 / math.sqrt(head_size)
    spec = pl.BlockSpec((1, width, head_size), lambda r, t: (r, t, 0))
    pairs = rows * len(qs) * tokens * list_len * part
    return rows, tokens // width, head_size, list_len * part, scale, math.log2(math.e) * scale, spec, pairs


def cost(pairs, head_size, dots, tensors):
    return pl.CostEstimate(
        flops=2 * dots * pairs * head_size, bytes_accessed=2 * sum(x.size for x in tensors), transcendentals=pairs
    )


def row_stats(table, arrived, qs, ts, steps, sections, list_len, part, width):
    rows, tiles, head_size, keys, _, scale2, _, pairs = plan(qs, list_len, part, width)
    spec = pl.BlockSpec((1, tiles * width, head_size), lambda r: (r, 0, 0))
    return pl.pallas_call(
        functools.partial(stats_kernel, list_len, part, scale2, rows, width, sections, steps),
        out_shape=jax.ShapeDtypeStruct((3 * sections * rows * tiles, width), f32),
        grid=(rows,),
        in_specs=[SMEM, VMEM] + [spec] * (2 * len(steps)),
        out_specs=VMEM,
        scratch_shapes=[pltpu.VMEM((keys, head_size), bf16)] * 2,
        cost_estimate=cost(pairs, head_size, 2, qs + ts),
        name="stats",
    )(table, arrived, *qs, *ts)


def far_stats(table, arrived, near, q, t, step, sections, list_len, part, width):
    rows, _, head_size, keys, _, scale2, _, pairs = plan((q,), list_len, part, width)
    return pl.pallas_call(
        functools.partial(far_kernel, list_len, part, scale2, width, sections, step),
        out_shape=jax.ShapeDtypeStruct((sections,) + near.shape, f32),
        in_specs=[SMEM, VMEM, VMEM] + [pl.BlockSpec(memory_space=pl.ANY)] * 2,
        out_specs=VMEM,
        scratch_shapes=[pltpu.VMEM(near.shape, f32)]
        + [pltpu.VMEM((rows, keys, head_size), bf16)] * 2
        + [pltpu.VMEM(q.shape, bf16)] * 2
        + [pltpu.SemaphoreType.DMA((rows, 2))],
        cost_estimate=cost(pairs, head_size, 2, (q, t)),
        compiler_params=pltpu.CompilerParams(vmem_limit_bytes=67043328),
        name="far",
    )(table, arrived, near, q, t)


def row_grads(table, arrived, stats, qs, ts, steps, list_len, part, width):
    rows, tiles, head_size, keys, scale, scale2, spec, pairs = plan(qs, list_len, part, width)
    sections = len(steps)
    return pl.pallas_call(
        functools.partial(grad_kernel, list_len, part, scale, scale2, rows, tiles, steps),
        out_shape=(
            jax.ShapeDtypeStruct(arrived.shape, bf16),
            jax.ShapeDtypeStruct((2 * sections * rows * tiles, width), f32),
        ),
        grid=(rows, tiles),
        in_specs=[SMEM, VMEM, VMEM] + [spec] * (2 * sections),
        out_specs=(VMEM, VMEM),
        scratch_shapes=[pltpu.VMEM((keys, head_size), bf16)] * 2 + [pltpu.VMEM((keys, head_size), f32)] * 2,
        cost_estimate=cost(pairs, head_size, 4, qs + ts),
        name="grads",
    )(table, arrived, stats, *qs, *ts)


def row_attend(table, arrived, totals, qs, steps, list_len, part, width):
    rows, tiles, head_size, keys, _, scale2, spec, pairs = plan(qs, list_len, part, width)
    sections = len(steps)
    return pl.pallas_call(
        functools.partial(attend_kernel, list_len, part, scale2, rows, tiles, steps),
        out_shape=[jax.ShapeDtypeStruct(qs[0].shape, bf16)] * sections,
        grid=(rows, tiles),
        in_specs=[SMEM, VMEM, VMEM] + [spec] * sections,
        out_specs=[spec] * sections,
        scratch_shapes=[pltpu.VMEM((keys, head_size), bf16)] * 2 + [pltpu.VMEM((head_size, keys), bf16)],
        cost_estimate=cost(pairs, head_size, 2, qs + qs),
        name="attend",
    )(table, arrived, totals, *qs)


def collect_kernel(slot_ref, returned_ref, grad_ref, square_ref):
    step = pl.program_id(0)
    group = returned_ref.shape[0]

    @pl.when(step == 0)
    def _():
        grad_ref[...] = jnp.zeros_like(grad_ref)

    for j in range(group):
        d = slot_ref[step * group + j, 0, 0]

        @pl.when(d >= 0)
        def _():
            grad_ref[d] = grad_ref[d] + returned_ref[j].astype(f32)

    @pl.when(step == pl.num_programs(0) - 1)
    def _():
        total = functools.reduce(jnp.add, [grad_ref[d] * grad_ref[d] for d in range(grad_ref.shape[0])])
        total = jnp.sum(total, axis=0, keepdims=True)
        for j in range(square_ref.shape[0]):
            square_ref[j] = total


def collect(slots, returned, docs):
    readers, rows, lanes = returned.shape
    group = max(1, readers // 4)
    return pl.pallas_call(
        collect_kernel,
        out_shape=(
            jax.ShapeDtypeStruct((docs, rows, lanes), f32),
            jax.ShapeDtypeStruct((readers, 1, lanes), f32),
        ),
        grid=(readers // group,),
        in_specs=[SMEM, pl.BlockSpec((group, rows, lanes), lambda i: (i, 0, 0))],
        out_specs=(VMEM, VMEM),
        compiler_params=small(8),
        name="collect",
    )(slots, returned)


def fold_kernel(square_ref, out_ref):
    total = functools.reduce(jnp.add, [square_ref[j] for j in range(square_ref.shape[0])])
    for j in range(out_ref.shape[0]):
        out_ref[j] = total


def fold(square, count):
    return pl.pallas_call(
        fold_kernel,
        out_shape=jax.ShapeDtypeStruct((count,) + square.shape[1:], f32),
        in_specs=[VMEM],
        out_specs=VMEM,
        compiler_params=small(2),
        name="fold",
    )(square)


def update_kernel(clip_limit, square_ref, grad_ref, cache_ref, momentum_ref, new_cache_ref, new_momentum_ref):
    total = functools.reduce(jnp.add, [square_ref[j] for j in range(square_ref.shape[0])])
    norm = jnp.sqrt(jnp.sum(total, axis=1, keepdims=True))
    factor = clip_limit / jnp.maximum(norm, clip_limit)
    docs, rows, _ = grad_ref.shape
    half = rows // 2

    def one(d, _):
        for kind in range(2):
            at = (d, pl.ds(kind, half, stride=2), slice(None))
            new_momentum_ref[at] = momentum_decay * momentum_ref[at] + factor * grad_ref[d, kind * half : (kind + 1) * half, :]
        new_cache_ref[d] = (cache_ref[d].astype(f32) - step_rate * new_momentum_ref[d]).astype(bf16)
        return 0

    lax.fori_loop(0, docs, one, 0)


def update(clip_limit, square, grad, cache, momentum):
    return pl.pallas_call(
        functools.partial(update_kernel, clip_limit),
        out_shape=(jax.ShapeDtypeStruct(cache.shape, bf16), jax.ShapeDtypeStruct(momentum.shape, f32)),
        in_specs=[VMEM] * 4,
        out_specs=(VMEM, VMEM),
        compiler_params=small(8),
        name="update",
    )(square, grad, cache, momentum)


def swap(x, axes):
    return lax.all_to_all(x, axes, split_axis=0, concat_axis=0, tiled=True)


def pass_on(x, ring):
    return lax.ppermute(x, "section", ring)


def body(queries, cotangent, cache, momentum, doc_lists, place):
    rows_dev, seq_len, head_count, kv_count, head_size = queries.shape
    doc_dev, len_part = cache.shape[:2]
    doc_total = place.shape[0]
    owners = doc_total // doc_dev
    list_len = doc_lists.shape[1]
    sections = lax.axis_size("section")
    tokens = seq_len * head_count

    q_own = queries.reshape(rows_dev, tokens, head_size)
    t_own = cotangent.reshape(rows_dev, tokens, head_size)
    up = [(i, (i + 1) % sections) for i in range(sections)]
    down = [(i, (i - 1) % sections) for i in range(sections)]
    across = [(i, (i + 2) % sections) for i in range(sections)]
    q_prev, t_next = pass_on(q_own, up), pass_on(t_own, down)
    q_next, t_prev = pass_on(q_own, down), pass_on(t_own, up)
    q_far, t_far = pass_on(q_prev, up), pass_on(t_next, down)
    qs, ts = (q_own, q_prev, q_next, q_far), (t_own, t_prev, t_next, t_far)
    steps = (0, 3, 1, 2)

    wanted, table = ask(doc_lists, place, owners, doc_dev)
    slots = swap(wanted, "doc")
    stored = cache.reshape(doc_dev, len_part * 2, head_size)
    outgoing = pick(slots, split(stored))
    arrived = swap(outgoing, "doc")

    width = 512
    near = row_stats(table, arrived, qs[:3], ts[:3], steps[:3], sections, list_len, len_part, width)
    stats = far_stats(table, arrived, near, qs[3], ts[3], steps[3], sections, list_len, len_part, width)
    stats = swap(stats, "section")
    parcel, totals = row_grads(table, arrived, stats, qs, ts, steps, list_len, len_part, width)
    own, to_prev, to_next, to_far = row_attend(table, arrived, totals, qs, steps, list_len, len_part, width)
    shares = (own, pass_on(to_prev, down), pass_on(to_next, up), pass_on(to_far, across))
    attention = sum(x.astype(f32) for x in shares).astype(bf16).reshape(queries.shape)

    returned = swap(parcel, "doc")
    gradient, square = collect(slots, returned, doc_dev)
    planes = sections * lax.axis_size("mp")
    square = fold(swap(square, "doc"), planes)
    square = swap(square, ("section", "mp"))
    entry_count = doc_total * len_part * planes * kv_count * 2 * head_size
    clip_limit = clip_level * math.sqrt(entry_count)
    new_cache, new_momentum = update(
        clip_limit, square, gradient, stored, momentum.reshape(doc_dev, len_part * 2, head_size)
    )
    return (attention, new_cache.reshape(cache.shape), new_momentum.reshape(momentum.shape))


def solution(mesh):
    in_specs = (
        P("doc", None, "section", "mp", None),
        P("doc", None, "section", "mp", None),
        P("doc", "section", "mp", None, None),
        P("doc", "section", "mp", None, None),
        P("doc", None),
        P(),
    )
    out_specs = (
        P("doc", None, "section", "mp", None),
        P("doc", "section", "mp", None, None),
        P("doc", "section", "mp", None, None),
    )

    return jax.shard_map(body, mesh=mesh, in_specs=in_specs, out_specs=out_specs, check_vma=False)
```
